32 devices in a mesh: groups: 2 (over y), seq: 8 (over z, x), tensor: 2 (over core).
Axes of the slice: x: 2, y: 2, z: 4, core: 2. Of those that a mesh axis runs over, the one named last changes fastest.
Arguments:
- queries: bfloat16 [256, 3072], P(('groups', 'seq'), 'tensor'), parts along dimension 0, may hold values from -8 to 8
- keys: bfloat16 [16384, 3072], P(('groups', 'seq'), 'tensor'), parts along dimension 0, may hold values from -8 to 8
- values: bfloat16 [16384, 3072], P(('groups', 'seq'), 'tensor'), parts along dimension 0, may hold values from -6 to 6
Outputs:
- context: bfloat16 [256, 3072], P(('groups', 'seq'), 'tensor'), parts along dimension 0
The draws below stay inside these ranges and needn't reach their ends.
There are 2 independent parts, one for each index of `groups`. The reference program is written for one: setup_inputs(seed, part) draws one part's arguments, and reference() takes and returns one part's arrays. A program takes and returns all parts, laid end to end along the dimension named above; each array names one. Nothing has to cross between parts.
All inputs are finite; a program needn't handle non-finite values.
Results may differ from the reference program's by a relative error of at most 0.0029.
Values may be sent and summed in bfloat16 or wider, within the bound.
A program may use at most 64 MiB of HBM per device.

```python
import math
import jax
import jax.numpy as jnp
from jax import lax

HEADS = 12
HEAD_DIM = 256
KEYS_DEV = 1024
QUERIES = 128
KEYS = 8192
ATTN_WIDTH = 3072
N_SEQ = 8


def drawn_pair(key):
    total_keys = KEYS_DEV * N_SEQ
    columns = HEADS * HEAD_DIM
    query_seed = jax.random.fold_in(key, 11)
    key_seed = jax.random.fold_in(key, 23)
    query_vals = jnp.clip(2.0 * jax.random.normal(query_seed, (QUERIES, columns), jnp.float32), -8.0, 8.0)
    key_vals = jnp.clip(2.0 * jax.random.normal(key_seed, (total_keys, columns), jnp.float32), -8.0, 8.0)
    return (query_vals, key_vals)


def draw_queries(key, part):
    return drawn_pair(key)[0].astype(jnp.bfloat16)


def draw_keys(key, part):
    return drawn_pair(key)[1].astype(jnp.bfloat16)


def steps_of(key, dims, split, low, top_value):
    level, own = 1.0, jax.random.fold_in(key, 6)
    for position, parts in split:
        steps = jnp.exp(jax.random.uniform(jax.random.fold_in(own, position), (parts,), jnp.float32, low / len(split), top_value / len(split)))
        level = level * jnp.repeat(steps, dims[position] // parts).reshape([-1 if axis == position else 1 for axis in range(len(dims))])
    return level


def centred(key, dims, deviation, most, shards=(), dtype=jnp.bfloat16):
    level = steps_of(key, dims, shards, -0.22, 0.18) if shards else 1.0
    entries = jax.random.normal(key, dims, jnp.float32) * deviation * level
    return jnp.minimum(jnp.maximum(entries, -most), most).astype(dtype)


def setup_inputs(seed: int = 0, part: int = 0) -> dict:
    splits = jax.random.split(jax.random.key(seed), 4)
    own_keys = jax.random.split(jax.random.fold_in(splits[3], part), 4)
    queries = draw_queries(jax.random.fold_in(jax.random.fold_in(splits[3], part), 71), part)
    keys = draw_keys(jax.random.fold_in(jax.random.fold_in(splits[3], part), 71), part)
    values = centred(own_keys[2], (KEYS, ATTN_WIDTH), 1.0, 6.0, ((0, 8), (1, 2)))
    return {"queries": queries, "keys": keys, "values": values}


def reference(queries, keys, values):
    query_count = queries.shape[0]
    score_factor = 1.0 / math.sqrt(HEAD_DIM)
    query_heads = queries.astype(jnp.float32).reshape(query_count, HEADS, HEAD_DIM)
    key_blocks = keys.reshape(N_SEQ, KEYS_DEV, HEADS, HEAD_DIM)
    value_blocks = values.reshape(N_SEQ, KEYS_DEV, HEADS, HEAD_DIM)

    def visit_block(carried, block_pair):
        overall, numerator, denominator = carried
        key_block, value_block = block_pair
        scores = jnp.einsum('qhd,khd->qhk', query_heads, key_block.astype(jnp.float32)) * score_factor
        block_peak = lax.optimization_barrier(jnp.max(scores, axis=-1))
        weights = jnp.exp(scores - block_peak[..., None])
        rounded = lax.optimization_barrier(weights.astype(jnp.bfloat16)).astype(jnp.float32)
        block_sums = lax.optimization_barrier(jnp.sum(weights, axis=-1))
        block_context = jnp.einsum('qhk,khd->qhd', rounded, value_block.astype(jnp.float32))
        updated = jnp.maximum(overall, block_peak)
        shrink = jnp.exp(overall - updated)
        stretch = jnp.exp(block_peak - updated)
        numerator = numerator * shrink[..., None] + block_context * stretch[..., None]
        denominator = denominator * shrink + block_sums * stretch
        return ((updated, numerator, denominator), None)
    start = (jnp.full((query_count, HEADS), -1e+30, jnp.float32), jnp.zeros((query_count, HEADS, HEAD_DIM), jnp.float32), jnp.zeros((query_count, HEADS), jnp.float32))
    finished, _ = lax.scan(visit_block, start, (key_blocks, value_blocks))
    numerator = finished[1]
    denominator = finished[2]
    return (numerator / denominator[..., None]).reshape(query_count, HEADS * HEAD_DIM).astype(jnp.bfloat16)
```

```python
import functools
import math

import jax
import jax.numpy as jnp
from jax import lax
from jax.experimental import pallas as pl
from jax.experimental.pallas import tpu as pltpu
from jax.sharding import PartitionSpec as P

HEAD_DIM = 256
LANES = 128
LINK = jnp.bfloat16


def over(count, step):
    if count <= 16:
        for index in range(count):
            step(index)
    else:
        lax.fori_loop(0, count, lambda index, _: (step(index), 0)[1], 0)


def encode(x):
    squared = x * x
    return (squared * (x * jnp.abs(x))).astype(LINK)


def decode(y):
    y = y.astype(jnp.float32)
    root = jnp.sqrt(jnp.sqrt(jnp.abs(y)))
    return jnp.where(y < 0, -root, root)


def kernel(
    n, q_ref, k_hbm, v_hbm, o_ref, qall, kbuf, vbuf, ctx, stat, rctx, rstat,
    ksem, vsem, qsend, qrecv, csend, crecv, ssend, srecv,
):
    rows, columns = q_ref.shape
    heads = columns // HEAD_DIM
    factor = 1.0 / math.sqrt(HEAD_DIM)
    me = lax.axis_index("seq")

    def cols(h):
        return pl.ds(h * HEAD_DIM, HEAD_DIM)

    def k_copy(h):
        return pltpu.make_async_copy(k_hbm.at[:, cols(h)], kbuf.at[h], ksem.at[h])

    def v_copy(h):
        return pltpu.make_async_copy(v_hbm.at[:, cols(h)], vbuf.at[h], vsem.at[h])

    def peer(d):
        return {"seq": lax.rem(me + d + 1, n)}

    def source(d):
        return lax.rem(me + n - d - 1, n)

    def q_send(d):
        return pltpu.make_async_remote_copy(
            src_ref=q_ref, dst_ref=qall.at[me], send_sem=qsend.at[d], recv_sem=qrecv.at[d],
            device_id=peer(d), device_id_type=pl.DeviceIdType.MESH,
        )

    def c_send(d, h):
        return pltpu.make_async_remote_copy(
            src_ref=ctx.at[h, peer(d)["seq"]], dst_ref=rctx.at[h, me],
            send_sem=csend.at[h, d], recv_sem=crecv.at[h, d],
            device_id=peer(d), device_id_type=pl.DeviceIdType.MESH,
        )

    def s_send(d):
        return pltpu.make_async_remote_copy(
            src_ref=stat.at[peer(d)["seq"]], dst_ref=rstat.at[me],
            send_sem=ssend.at[d], recv_sem=srecv.at[d],
            device_id=peer(d), device_id_type=pl.DeviceIdType.MESH,
        )

    for h in range(heads):
        k_copy(h).start()
        v_copy(h).start()

    barrier = pltpu.get_barrier_semaphore()
    over(n - 1, lambda d: pl.semaphore_signal(
        barrier, inc=1, device_id=peer(d), device_id_type=pl.DeviceIdType.MESH))
    pl.semaphore_wait(barrier, n - 1)

    over(n - 1, lambda d: q_send(d).start())
    qall[me] = q_ref[...]
    over(n - 1, lambda d: q_send(d).wait_recv())

    group = min(n, 8)

    def attend(h, g):
        base = g * group
        query = qall[pl.ds(base, group), :, cols(h)].reshape(group * rows, HEAD_DIM)
        scores = lax.dot_general(
            query, kbuf[h], (((1,), (1,)), ((), ())), preferred_element_type=jnp.float32
        )
        peak = jnp.max(scores, axis=-1, keepdims=True)
        weights = jnp.exp((scores - peak) * factor)
        sums = jnp.sum(weights, axis=-1, keepdims=True)
        context = jnp.dot(
            weights.astype(jnp.bfloat16), vbuf[h], preferred_element_type=jnp.float32
        )
        size = jnp.max(jnp.abs(context), axis=-1, keepdims=True)
        size = jnp.maximum(size, 1e-30)
        ctx[h, pl.ds(base, group)] = encode(context / size).reshape(group, rows, HEAD_DIM)
        for place, value in ((0, peak * factor), (heads, sums), (2 * heads, size)):
            stat[pl.ds(base, group), :, pl.ds(place + h, 1)] = value.reshape(group, rows, 1)

    for h in range(heads):
        k_copy(h).wait()
        v_copy(h).wait()
        over(n // group, functools.partial(attend, h))
        over(n - 1, lambda d: c_send(d, h).start())
    over(n - 1, lambda d: s_send(d).start())
    rstat[me] = stat[me]
    for h in range(heads):
        rctx[h, me] = ctx[h, me]
    over(n - 1, lambda d: s_send(d).wait_recv())

    peaks = rstat[...]
    top = jnp.max(peaks, axis=0, keepdims=True)
    shrink = jnp.exp(peaks - top)
    for h in range(heads):
        over(n - 1, lambda d: c_send(d, h).wait_recv())
        part = shrink[:, :, h : h + 1]
        total = jnp.sum(part * peaks[:, :, heads + h : heads + h + 1], axis=0)
        scale = part * peaks[:, :, 2 * heads + h : 2 * heads + h + 1]
        numerator = jnp.sum(decode(rctx[h]) * scale, axis=0)
        o_ref[:, cols(h)] = (numerator / total).astype(o_ref.dtype)

    over(n - 1, lambda d: q_send(d).wait_send())
    over(n - 1, lambda d: s_send(d).wait_send())
    for h in range(heads):
        over(n - 1, lambda d: c_send(d, h).wait_send())


def body(n, queries, keys, values):
    rows, columns = queries.shape
    depth = keys.shape[0]
    heads = columns // HEAD_DIM
    dma = pltpu.SemaphoreType.DMA
    vmem = pl.BlockSpec(memory_space=pltpu.VMEM)
    return pl.pallas_call(
        functools.partial(kernel, n),
        out_shape=jax.ShapeDtypeStruct((rows, columns), jnp.bfloat16),
        in_specs=[vmem, pl.BlockSpec(memory_space=pl.ANY), pl.BlockSpec(memory_space=pl.ANY)],
        out_specs=vmem,
        scratch_shapes=[
            pltpu.VMEM((n, rows, columns), jnp.bfloat16),
            pltpu.VMEM((heads, depth, HEAD_DIM), jnp.bfloat16),
            pltpu.VMEM((heads, depth, HEAD_DIM), jnp.bfloat16),
            pltpu.VMEM((heads, n, rows, HEAD_DIM), LINK),
            pltpu.VMEM((n, rows, LANES), jnp.float32),
            pltpu.VMEM((heads, n, rows, HEAD_DIM), LINK),
            pltpu.VMEM((n, rows, LANES), jnp.float32),
            dma((heads,)), dma((heads,)),
            dma((n - 1,)), dma((n - 1,)),
            dma((heads, n - 1)), dma((heads, n - 1)),
            dma((n - 1,)), dma((n - 1,)),
        ],
        compiler_params=pltpu.CompilerParams(
            collective_id=0, has_side_effects=True, vmem_limit_bytes=48 * 1024 * 1024
        ),
        name="attend",
    )(queries, keys, values)


def solution(mesh):
    spec = P(("groups", "seq"), "tensor")
    return jax.shard_map(
        functools.partial(body, mesh.shape["seq"]),
        mesh=mesh,
        in_specs=(spec, spec, spec),
        out_specs=spec,
        check_vma=False,
    )
```

```python
import functools
import math

import jax
import jax.numpy as jnp
from jax import lax
from jax.experimental import pallas as pl
from jax.experimental.pallas import tpu as pltpu
from jax.sharding import PartitionSpec as P

HEAD_DIM = 256
LANES = 128
LINK = jnp.bfloat16
CHUNK = 3
RAISE = 2.0**28
LOWER = 2.0**-28


def encode(x):
    x = x * RAISE
    squared = x * x
    return (squared * (x * jnp.abs(x))).astype(LINK)


def decode(y):
    y = y.astype(jnp.float32)
    root = jnp.sqrt(jnp.sqrt(jnp.abs(y))) * LOWER
    return jnp.where(y < 0, -root, root)


def over(start, stop, step):
    if stop - start <= 16:
        for index in range(start, stop):
            step(index)
    else:
        lax.fori_loop(start, stop, lambda index, _: (step(index), 0)[1], 0)


def kernel(
    n, q_ref, k_hbm, v_hbm, o_ref, qall, kbuf, vbuf, local, stat, xout, xin, tout, tin,
    zout, zin, zstat, ystat,
    ksem, vsem, qzs, qzr, qxs, qxr, xs, xr, ts, tr, zs, zr, ys, yr,
):
    rows, columns = q_ref.shape
    heads = columns // HEAD_DIM
    chunks = heads // CHUNK
    factor = 1.0 / math.sqrt(HEAD_DIM)
    m = n // 2
    me = lax.axis_index("seq")
    place = me // 2
    side = lax.rem(me, 2)
    other = 1 - side
    pair = 2 * place + other

    def ahead(k):
        return lax.rem(place + k, m)

    def behind(k):
        return lax.rem(place + m - k, m)

    def cols(h):
        return pl.ds(h * HEAD_DIM, HEAD_DIM)

    def span(c):
        return pl.ds(c * CHUNK * HEAD_DIM, CHUNK * HEAD_DIM)

    def k_copy(h):
        return pltpu.make_async_copy(k_hbm.at[:, cols(h)], kbuf.at[h], ksem.at[h])

    def v_copy(h):
        return pltpu.make_async_copy(v_hbm.at[:, cols(h)], vbuf.at[h], vsem.at[h])

    def remote(src, dst, send, recv, to):
        return pltpu.make_async_remote_copy(
            src_ref=src, dst_ref=dst, send_sem=send, recv_sem=recv,
            device_id={"seq": to}, device_id_type=pl.DeviceIdType.MESH,
        )

    def column(k):
        return 2 * ahead(k) + side

    def qz(c, k):
        return remote(q_ref.at[:, span(c)], qall.at[side, place, :, span(c)],
                      qzs.at[c, k], qzr.at[c, k], column(k))

    def qx_own(c):
        return remote(q_ref.at[:, span(c)], qall.at[side, place, :, span(c)],
                      qxs.at[c, 0], qxr.at[c, 0], pair)

    def qx(c, k):
        ref = qall.at[side, behind(k), :, span(c)]
        return remote(ref, ref, qxs.at[c, k], qxr.at[c, k], pair)

    def x_send(c):
        return remote(xout.at[c], xin.at[c], xs.at[c], xr.at[c], pair)

    def t_send(c):
        return remote(tout.at[c], tin.at[c], ts.at[c], tr.at[c], pair)

    def z_send(c, k):
        return remote(zout.at[c, ahead(k)], zin.at[c, place], zs.at[c, k], zr.at[c, k], column(k))

    def y_send(k):
        return remote(zstat.at[ahead(k)], ystat.at[place], ys.at[k], yr.at[k], column(k))

    barrier = pltpu.get_barrier_semaphore()

    def greet(to):
        pl.semaphore_signal(
            barrier, inc=1, device_id={"seq": to}, device_id_type=pl.DeviceIdType.MESH)

    over(1, m, lambda k: greet(column(k)))
    greet(pair)
    for h in range(heads):
        k_copy(h).start()
        v_copy(h).start()
    qall[side, place] = q_ref[...]
    stat[...] = jnp.zeros_like(stat)
    zstat[...] = jnp.zeros_like(zstat)
    pl.semaphore_wait(barrier, m)

    for c in range(chunks):
        over(1, m, lambda k: qz(c, k).start())
        qx_own(c).start()
    for h in range(heads):
        k_copy(h).wait()
        v_copy(h).wait()

    group = min(m, 4)
    count = 2 * group * rows

    def forward(c):
        def step(k):
            qz(c, k).wait_recv()
            qx(c, k).start()
        over(1, m, step)

    def attend(c, g):
        base = g * group
        hs = range(c * CHUNK, (c + 1) * CHUNK)
        scores = [
            lax.dot_general(
                qall[:, pl.ds(base, group), :, cols(h)].reshape(count, HEAD_DIM),
                kbuf[h], (((1,), (1,)), ((), ())), preferred_element_type=jnp.float32,
            )
            for h in hs
        ]
        for h, score in zip(hs, scores):
            peak = jnp.max(score, axis=-1, keepdims=True)
            weights = jnp.exp((score - peak) * factor)
            sums = jnp.sum(weights, axis=-1, keepdims=True)
            context = jnp.dot(
                weights.astype(jnp.bfloat16), vbuf[h], preferred_element_type=jnp.float32
            )
            local[h, :, pl.ds(base, group)] = (context / sums).reshape(2, group, rows, HEAD_DIM)
            stat[:, pl.ds(base, group), :, pl.ds(h, 1)] = (
                peak * factor + jnp.log(sums)
            ).reshape(2, group, rows, 1)

    def compute(c):
        qx_own(c).wait_recv()
        over(1, m, lambda k: qx(c, k).wait_recv())
        over(0, m // group, functools.partial(attend, c))
        for i in range(CHUNK):
            xout[c, i] = encode(local[c * CHUNK + i, other])
        x_send(c).start()
        flat = stat[other].reshape(m * rows, LANES)
        tout[c] = flat.T[: tout.shape[1]]
        t_send(c).start()

    def merge(c):
        t_send(c).wait_recv()
        flat = tin[c].T
        x_send(c).wait_recv()
        for i in range(CHUNK):
            h = c * CHUNK + i
            mine = stat[side, :, :, pl.ds(h, 1)]
            theirs = flat[:, h : h + 1].reshape(m, rows, 1)
            top = jnp.maximum(mine, theirs)
            total = top + jnp.log(jnp.exp(mine - top) + jnp.exp(theirs - top))
            value = local[h, side] * jnp.exp(mine - total) + decode(xin[c, i]) * jnp.exp(theirs - total)
            local[h, side] = value
            zstat[:, :, pl.ds(h, 1)] = total
            coded = encode(value)
            zout[c, :, i] = coded
        over(1, m, lambda k: z_send(c, k).start())

    forward(0)
    for c in range(chunks):
        if c + 1 < chunks:
            forward(c + 1)
        compute(c)
        if c > 0:
            merge(c - 1)
    merge(chunks - 1)
    over(1, m, lambda k: y_send(k).start())

    ystat[place] = zstat[place]
    over(1, m, lambda k: y_send(k).wait_recv())
    peaks = ystat[...]
    top = jnp.max(peaks, axis=0, keepdims=True)
    share = jnp.exp(peaks - top)
    share = share / jnp.sum(share, axis=0, keepdims=True)
    ystat[...] = share
    for c in range(chunks):
        over(1, m, lambda k: z_send(c, k).wait_recv())
        for i in range(CHUNK):
            h = c * CHUNK + i
            result = local[h, side, place] * ystat[place, :, pl.ds(h, 1)]
            for k in range(1, m):
                b = behind(k)
                result = result + decode(zin[c, b, i]) * ystat[b, :, pl.ds(h, 1)]
            o_ref[:, cols(h)] = result.astype(o_ref.dtype)

    for c in range(chunks):
        over(1, m, lambda k: qz(c, k).wait_send())
        qx_own(c).wait_send()
        over(1, m, lambda k: qx(c, k).wait_send())
        x_send(c).wait_send()
        t_send(c).wait_send()
        over(1, m, lambda k: z_send(c, k).wait_send())
    over(1, m, lambda k: y_send(k).wait_send())


def body(n, queries, keys, values):
    rows, columns = queries.shape
    depth = keys.shape[0]
    heads = columns // HEAD_DIM
    chunks = heads // CHUNK
    m = n // 2
    high = 8 * pl.cdiv(heads, 8)
    dma = pltpu.SemaphoreType.DMA
    vmem = pl.BlockSpec(memory_space=pltpu.VMEM)
    hbm = pl.BlockSpec(memory_space=pltpu.HBM)
    return pl.pallas_call(
        functools.partial(kernel, n),
        out_shape=jax.ShapeDtypeStruct((rows, columns), jnp.bfloat16),
        in_specs=[vmem, hbm, hbm],
        out_specs=vmem,
        scratch_shapes=[
            pltpu.VMEM((2, m, rows, columns), jnp.bfloat16),
            pltpu.VMEM((heads, depth, HEAD_DIM), jnp.bfloat16),
            pltpu.VMEM((heads, depth, HEAD_DIM), jnp.bfloat16),
            pltpu.VMEM((heads, 2, m, rows, HEAD_DIM), jnp.float32),
            pltpu.VMEM((2, m, rows, LANES), jnp.float32),
            pltpu.VMEM((chunks, CHUNK, m, rows, HEAD_DIM), LINK),
            pltpu.VMEM((chunks, CHUNK, m, rows, HEAD_DIM), LINK),
            pltpu.VMEM((chunks, high, m * rows), jnp.float32),
            pltpu.VMEM((chunks, high, m * rows), jnp.float32),
            pltpu.VMEM((chunks, m, CHUNK, rows, HEAD_DIM), LINK),
            pltpu.VMEM((chunks, m, CHUNK, rows, HEAD_DIM), LINK),
            pltpu.VMEM((m, rows, LANES), jnp.float32),
            pltpu.VMEM((m, rows, LANES), jnp.float32),
            dma((heads,)), dma((heads,)),
            dma((chunks, m)), dma((chunks, m)),
            dma((chunks, m)), dma((chunks, m)),
            dma((chunks,)), dma((chunks,)),
            dma((chunks,)), dma((chunks,)),
            dma((chunks, m)), dma((chunks, m)),
            dma((m,)), dma((m,)),
        ],
        compiler_params=pltpu.CompilerParams(
            collective_id=0, has_side_effects=True, vmem_limit_bytes=48 * 1024 * 1024
        ),
        name="attend",
    )(queries, keys, values)


def solution(mesh):
    spec = P(("groups", "seq"), "tensor")
    return jax.shard_map(
        functools.partial(body, mesh.shape["seq"]),
        mesh=mesh,
        in_specs=(spec, spec, spec),
        out_specs=spec,
        check_vma=False,
    )
```

```python
import functools
import math

import jax
import jax.numpy as jnp
from jax import lax
from jax.experimental import pallas as pl
from jax.experimental.pallas import tpu as pltpu
from jax.sharding import PartitionSpec as P

HEAD_DIM = 256
LANES = 128
LINK = jnp.bfloat16
SIZES = (2, 2, 2)
AHEAD = 2
LAG = 3
RAISE = 2.0**28
LOWER = 2.0**-28


def encode(x):
    x = x * RAISE
    squared = x * x
    return (squared * (x * jnp.abs(x))).astype(LINK)


def decode(y):
    y = y.astype(jnp.float32)
    root = jnp.sqrt(jnp.sqrt(jnp.abs(y))) * LOWER
    return jnp.where(y < 0, -root, root)


def over(start, stop, step):
    if stop - start <= 16:
        for index in range(start, stop):
            step(index)
    else:
        lax.fori_loop(start, stop, lambda index, _: (step(index), 0)[1], 0)


def split_heads(heads):
    return SIZES if sum(SIZES) == heads else (heads,)


def kernel(
    n, q_ref, k_hbm, v_hbm, o_ref, qall, kbuf, vbuf, local, stat, xout, xin, tout, tin,
    zout, zin, zstat, ystat,
    ksem, vsem, qzs, qzr, qxs, qxr, xs, xr, ts, tr, zs, zr, ys, yr,
):
    rows, columns = q_ref.shape
    heads = columns // HEAD_DIM
    sizes = split_heads(heads)
    starts = [sum(sizes[:c]) for c in range(len(sizes))]
    chunks = len(sizes)
    factor = 1.0 / math.sqrt(HEAD_DIM)
    m = n // 2
    me = lax.axis_index("seq")
    place = me // 2
    side = lax.rem(me, 2)
    other = 1 - side
    pair = 2 * place + other

    def ahead(k):
        return lax.rem(place + k, m)

    def behind(k):
        return lax.rem(place + m - k, m)

    def cols(h):
        return pl.ds(h * HEAD_DIM, HEAD_DIM)

    def span(c):
        return pl.ds(starts[c] * HEAD_DIM, sizes[c] * HEAD_DIM)

    def k_copy(h):
        return pltpu.make_async_copy(k_hbm.at[:, cols(h)], kbuf.at[h], ksem.at[h])

    def v_copy(h):
        return pltpu.make_async_copy(v_hbm.at[:, cols(h)], vbuf.at[h], vsem.at[h])

    def remote(src, dst, send, recv, to):
        return pltpu.make_async_remote_copy(
            src_ref=src, dst_ref=dst, send_sem=send, recv_sem=recv,
            device_id={"seq": to}, device_id_type=pl.DeviceIdType.MESH,
        )

    def column(k):
        return 2 * ahead(k) + side

    def qz(c, k):
        return remote(q_ref.at[:, span(c)], qall.at[side, place, :, span(c)],
                      qzs.at[c, k], qzr.at[c, k], column(k))

    def qx_own(c):
        return remote(q_ref.at[:, span(c)], qall.at[side, place, :, span(c)],
                      qxs.at[c, 0], qxr.at[c, 0], pair)

    def qx(c, k):
        ref = qall.at[side, behind(k), :, span(c)]
        return remote(ref, ref, qxs.at[c, k], qxr.at[c, k], pair)

    def x_send(c):
        part = pl.ds(starts[c], sizes[c])
        return remote(xout.at[part], xin.at[part], xs.at[c], xr.at[c], pair)

    def t_send(c):
        return remote(tout.at[c], tin.at[c], ts.at[c], tr.at[c], pair)

    def z_send(c, k):
        part = pl.ds(starts[c], sizes[c])
        return remote(zout.at[ahead(k), part], zin.at[place, part], zs.at[c, k], zr.at[c, k], column(k))

    def y_send(k):
        return remote(zstat.at[ahead(k)], ystat.at[place], ys.at[k], yr.at[k], column(k))

    barrier = pltpu.get_barrier_semaphore()

    def greet(to):
        pl.semaphore_signal(
            barrier, inc=1, device_id={"seq": to}, device_id_type=pl.DeviceIdType.MESH)

    over(1, m, lambda k: greet(column(k)))
    greet(pair)
    for h in range(heads):
        k_copy(h).start()
        v_copy(h).start()
    qall[side, place] = q_ref[...]
    stat[...] = jnp.zeros_like(stat)
    zstat[...] = jnp.zeros_like(zstat)
    pl.semaphore_wait(barrier, m)

    for c in range(chunks):
        over(1, m, lambda k: qz(c, k).start())
        qx_own(c).start()
    for h in range(heads):
        k_copy(h).wait()
        v_copy(h).wait()

    group = min(m, 4)
    count = 2 * group * rows

    def forward(c):
        def step(k):
            qz(c, k).wait_recv()
            qx(c, k).start()
        over(1, m, step)

    def attend(c, g):
        base = g * group
        hs = range(starts[c], starts[c] + sizes[c])
        scores = [
            lax.dot_general(
                qall[:, pl.ds(base, group), :, cols(h)].reshape(count, HEAD_DIM),
                kbuf[h], (((1,), (1,)), ((), ())), preferred_element_type=jnp.float32,
            )
            for h in hs
        ]
        for h, score in zip(hs, scores):
            peak = jnp.max(score, axis=-1, keepdims=True)
            weights = jnp.exp((score - peak) * factor)
            sums = jnp.sum(weights, axis=-1, keepdims=True)
            context = jnp.dot(
                weights.astype(jnp.bfloat16), vbuf[h], preferred_element_type=jnp.float32
            )
            local[h, :, pl.ds(base, group)] = (context / sums).reshape(2, group, rows, HEAD_DIM)
            stat[:, pl.ds(base, group), :, pl.ds(h, 1)] = (
                peak * factor + jnp.log(sums)
            ).reshape(2, group, rows, 1)

    def compute(c):
        qx_own(c).wait_recv()
        over(1, m, lambda k: qx(c, k).wait_recv())
        over(0, m // group, functools.partial(attend, c))
        flat = stat[other].reshape(m * rows, LANES)
        tout[c] = flat.T[: tout.shape[1]]
        t_send(c).start()
        for h in range(starts[c], starts[c] + sizes[c]):
            xout[h] = encode(local[h, other])
        x_send(c).start()

    def merge(c):
        t_send(c).wait_recv()
        flat = tin[c].T
        hs = range(starts[c], starts[c] + sizes[c])
        shares = []
        for h in hs:
            mine = stat[side, :, :, pl.ds(h, 1)]
            theirs = flat[:, h : h + 1].reshape(m, rows, 1)
            top = jnp.maximum(mine, theirs)
            total = top + jnp.log(jnp.exp(mine - top) + jnp.exp(theirs - top))
            zstat[:, :, pl.ds(h, 1)] = total
            shares.append((jnp.exp(mine - total), jnp.exp(theirs - total)))
        if c == chunks - 1:
            over(1, m, lambda k: y_send(k).start())
        x_send(c).wait_recv()
        for h, (mine, theirs) in zip(hs, shares):
            value = local[h, side] * mine + decode(xin[h]) * theirs
            local[h, side] = value
            zout[:, h] = encode(value)
        over(1, m, lambda k: z_send(c, k).start())

    for t in range(-AHEAD, chunks + LAG):
        if 0 <= t + AHEAD < chunks:
            forward(t + AHEAD)
        if 0 <= t < chunks:
            compute(t)
        if 0 <= t - LAG < chunks:
            merge(t - LAG)

    ystat[place] = zstat[place]
    over(1, m, lambda k: y_send(k).wait_recv())
    peaks = ystat[...]
    top = jnp.max(peaks, axis=0, keepdims=True)
    share = jnp.exp(peaks - top)
    share = share / jnp.sum(share, axis=0, keepdims=True)
    ystat[...] = share
    for c in range(chunks):
        over(1, m, lambda k: z_send(c, k).wait_recv())
        for h in range(starts[c], starts[c] + sizes[c]):
            result = local[h, side, place] * ystat[place, :, pl.ds(h, 1)]
            for k in range(1, m):
                b = behind(k)
                result = result + decode(zin[b, h]) * ystat[b, :, pl.ds(h, 1)]
            o_ref[:, cols(h)] = result.astype(o_ref.dtype)

    for c in range(chunks):
        over(1, m, lambda k: qz(c, k).wait_send())
        qx_own(c).wait_send()
        over(1, m, lambda k: qx(c, k).wait_send())
        x_send(c).wait_send()
        t_send(c).wait_send()
        over(1, m, lambda k: z_send(c, k).wait_send())
    over(1, m, lambda k: y_send(k).wait_send())


def body(n, queries, keys, values):
    rows, columns = queries.shape
    depth = keys.shape[0]
    heads = columns // HEAD_DIM
    chunks = len(split_heads(heads))
    m = n // 2
    high = 8 * pl.cdiv(heads, 8)
    dma = pltpu.SemaphoreType.DMA
    vmem = pl.BlockSpec(memory_space=pltpu.VMEM)
    hbm = pl.BlockSpec(memory_space=pltpu.HBM)
    return pl.pallas_call(
        functools.partial(kernel, n),
        out_shape=jax.ShapeDtypeStruct((rows, columns), jnp.bfloat16),
        in_specs=[vmem, hbm, hbm],
        out_specs=vmem,
        scratch_shapes=[
            pltpu.VMEM((2, m, rows, columns), jnp.bfloat16),
            pltpu.VMEM((heads, depth, HEAD_DIM), jnp.bfloat16),
            pltpu.VMEM((heads, depth, HEAD_DIM), jnp.bfloat16),
            pltpu.VMEM((heads, 2, m, rows, HEAD_DIM), jnp.float32),
            pltpu.VMEM((2, m, rows, LANES), jnp.float32),
            pltpu.VMEM((heads, m, rows, HEAD_DIM), LINK),
            pltpu.VMEM((heads, m, rows, HEAD_DIM), LINK),
            pltpu.VMEM((chunks, high, m * rows), jnp.float32),
            pltpu.VMEM((chunks, high, m * rows), jnp.float32),
            pltpu.VMEM((m, heads, rows, HEAD_DIM), LINK),
            pltpu.VMEM((m, heads, rows, HEAD_DIM), LINK),
            pltpu.VMEM((m, rows, LANES), jnp.float32),
            pltpu.VMEM((m, rows, LANES), jnp.float32),
            dma((heads,)), dma((heads,)),
            dma((chunks, m)), dma((chunks, m)),
            dma((chunks, m)), dma((chunks, m)),
            dma((chunks,)), dma((chunks,)),
            dma((chunks,)), dma((chunks,)),
            dma((chunks, m)), dma((chunks, m)),
            dma((m,)), dma((m,)),
        ],
        compiler_params=pltpu.CompilerParams(
            collective_id=0, has_side_effects=True, vmem_limit_bytes=48 * 1024 * 1024
        ),
        name="attend",
    )(queries, keys, values)


def solution(mesh):
    spec = P(("groups", "seq"), "tensor")
    return jax.shard_map(
        functools.partial(body, mesh.shape["seq"]),
        mesh=mesh,
        in_specs=(spec, spec, spec),
        out_specs=spec,
        check_vma=False,
    )
```

```python
import functools
import math

import jax
import jax.numpy as jnp
from jax import lax
from jax.experimental import pallas as pl
from jax.experimental.pallas import tpu as pltpu
from jax.sharding import PartitionSpec as P

HEAD_DIM = 256
LANES = 128
LINK = jnp.bfloat16
SIZES = (2, 2, 2)
AHEAD = 2
LAG = 3
RAISE = 2.0**28
LOWER = 2.0**-28


def encode(x):
    x = x * RAISE
    squared = x * x
    return (squared * (x * jnp.abs(x))).astype(LINK)


def decode(y):
    y = y.astype(jnp.float32)
    root = jnp.sqrt(jnp.sqrt(jnp.abs(y))) * LOWER
    return jnp.where(y < 0, -root, root)


def over(start, stop, step):
    if stop - start <= 16:
        for index in range(start, stop):
            step(index)
    else:
        lax.fori_loop(start, stop, lambda index, _: (step(index), 0)[1], 0)


def split_heads(heads):
    return SIZES if sum(SIZES) == heads else (heads,)


def kernel(
    n, q_ref, k_hbm, v_hbm, o_ref, qall, kbuf, vbuf, local, stat, xout, xin, tout, tin,
    zout, zin, zstat, ystat,
    ksem, vsem, qzs, qzr, qxs, qxr, xs, xr, ts, tr, zs, zr, ys, yr,
):
    rows, columns = q_ref.shape
    heads = columns // HEAD_DIM
    sizes = split_heads(heads)
    starts = [sum(sizes[:c]) for c in range(len(sizes))]
    chunks = len(sizes)
    factor = 1.0 / math.sqrt(HEAD_DIM)
    m = n // 2
    me = lax.axis_index("seq")
    place = me // 2
    side = lax.rem(me, 2)
    other = 1 - side
    pair = 2 * place + other

    def ahead(k):
        return lax.rem(place + k, m)

    def behind(k):
        return lax.rem(place + m - k, m)

    def cols(h):
        return pl.ds(h * HEAD_DIM, HEAD_DIM)

    def span(c):
        return pl.ds(starts[c] * HEAD_DIM, sizes[c] * HEAD_DIM)

    def k_copy(h):
        return pltpu.make_async_copy(k_hbm.at[:, cols(h)], kbuf.at[h], ksem.at[h])

    def v_copy(h):
        return pltpu.make_async_copy(v_hbm.at[:, cols(h)], vbuf.at[h], vsem.at[h])

    def remote(src, dst, send, recv, to):
        return pltpu.make_async_remote_copy(
            src_ref=src, dst_ref=dst, send_sem=send, recv_sem=recv,
            device_id={"seq": to}, device_id_type=pl.DeviceIdType.MESH,
        )

    def column(k):
        return 2 * ahead(k) + side

    def qz(c, k):
        return remote(q_ref.at[:, span(c)], qall.at[side, place, :, span(c)],
                      qzs.at[c, k], qzr.at[c, k], column(k))

    def qx_own(c):
        return remote(q_ref.at[:, span(c)], qall.at[side, place, :, span(c)],
                      qxs.at[c, 0], qxr.at[c, 0], pair)

    def qx(c, k):
        ref = qall.at[side, behind(k), :, span(c)]
        return remote(ref, ref, qxs.at[c, k], qxr.at[c, k], pair)

    def x_send(c):
        part = pl.ds(starts[c], sizes[c])
        return remote(xout.at[part], xin.at[part], xs.at[c], xr.at[c], pair)

    def t_send(c):
        return remote(tout.at[c], tin.at[c], ts.at[c], tr.at[c], pair)

    def z_send(c, k):
        part = pl.ds(starts[c], sizes[c])
        return remote(zout.at[ahead(k), part], zin.at[place, part], zs.at[c, k], zr.at[c, k], column(k))

    def y_send(k):
        return remote(zstat.at[ahead(k)], ystat.at[place], ys.at[k], yr.at[k], column(k))

    barrier = pltpu.get_barrier_semaphore()

    def greet(to):
        pl.semaphore_signal(
            barrier, inc=1, device_id={"seq": to}, device_id_type=pl.DeviceIdType.MESH)

    over(1, m, lambda k: greet(column(k)))
    greet(pair)
    for h in range(heads):
        k_copy(h).start()
        v_copy(h).start()
    qall[side, place] = q_ref[...]
    stat[...] = jnp.zeros_like(stat)
    zstat[...] = jnp.zeros_like(zstat)
    pl.semaphore_wait(barrier, m)

    for c in range(chunks):
        over(1, m, lambda k: qz(c, m - k).start())
        qx_own(c).start()
    for h in range(heads):
        k_copy(h).wait()
        v_copy(h).wait()

    group = min(m, 4)
    count = 2 * group * rows

    def forward(c):
        def step(k):
            qz(c, k).wait_recv()
            qx(c, k).start()
        over(1, m, step)

    def attend(c, g):
        base = g * group
        hs = range(starts[c], starts[c] + sizes[c])
        scores = [
            lax.dot_general(
                qall[:, pl.ds(base, group), :, cols(h)].reshape(count, HEAD_DIM),
                kbuf[h], (((1,), (1,)), ((), ())), preferred_element_type=jnp.float32,
            )
            for h in hs
        ]
        for h, score in zip(hs, scores):
            peak = jnp.max(score, axis=-1, keepdims=True)
            weights = jnp.exp((score - peak) * factor)
            sums = jnp.sum(weights, axis=-1, keepdims=True)
            context = jnp.dot(
                weights.astype(jnp.bfloat16), vbuf[h], preferred_element_type=jnp.float32
            )
            local[h, :, pl.ds(base, group)] = (context / sums).reshape(2, group, rows, HEAD_DIM)
            stat[:, pl.ds(base, group), :, pl.ds(h, 1)] = (
                peak * factor + jnp.log(sums)
            ).reshape(2, group, rows, 1)

    def compute(c):
        qx_own(c).wait_recv()
        over(1, m, lambda k: qx(c, k).wait_recv())
        over(0, m // group, functools.partial(attend, c))
        flat = stat[other].reshape(m * rows, LANES)
        tout[c] = flat.T[: tout.shape[1]]
        t_send(c).start()
        for h in range(starts[c], starts[c] + sizes[c]):
            xout[h] = encode(local[h, other])
        x_send(c).start()

    def merge(c):
        t_send(c).wait_recv()
        flat = tin[c].T
        hs = range(starts[c], starts[c] + sizes[c])
        shares = []
        for h in hs:
            mine = stat[side, :, :, pl.ds(h, 1)]
            theirs = flat[:, h : h + 1].reshape(m, rows, 1)
            top = jnp.maximum(mine, theirs)
            total = top + jnp.log(jnp.exp(mine - top) + jnp.exp(theirs - top))
            zstat[:, :, pl.ds(h, 1)] = total
            shares.append((jnp.exp(mine - total), jnp.exp(theirs - total)))
        if c == chunks - 1:
            over(1, m, lambda k: y_send(k).start())
        x_send(c).wait_recv()
        for h, (mine, theirs) in zip(hs, shares):
            value = local[h, side] * mine + decode(xin[h]) * theirs
            local[h, side] = value
            zout[:, h] = encode(value)
        over(1, m, lambda k: z_send(c, k).start())

    for t in range(-AHEAD, chunks + LAG):
        if 0 <= t + AHEAD < chunks:
            forward(t + AHEAD)
        if 0 <= t < chunks:
            compute(t)
        if 0 <= t - LAG < chunks:
            merge(t - LAG)

    ystat[place] = zstat[place]
    over(1, m, lambda k: y_send(k).wait_recv())
    peaks = ystat[...]
    top = jnp.max(peaks, axis=0, keepdims=True)
    share = jnp.exp(peaks - top)
    share = share / jnp.sum(share, axis=0, keepdims=True)
    ystat[...] = share
    for c in range(chunks):
        over(1, m, lambda k: z_send(c, k).wait_recv())
        for h in range(starts[c], starts[c] + sizes[c]):
            result = local[h, side, place] * ystat[place, :, pl.ds(h, 1)]
            for k in range(1, m):
                b = behind(k)
                result = result + decode(zin[b, h]) * ystat[b, :, pl.ds(h, 1)]
            o_ref[:, cols(h)] = result.astype(o_ref.dtype)

    for c in range(chunks):
        over(1, m, lambda k: qz(c, k).wait_send())
        qx_own(c).wait_send()
        over(1, m, lambda k: qx(c, k).wait_send())
        x_send(c).wait_send()
        t_send(c).wait_send()
        over(1, m, lambda k: z_send(c, k).wait_send())
    over(1, m, lambda k: y_send(k).wait_send())


def body(n, queries, keys, values):
    rows, columns = queries.shape
    depth = keys.shape[0]
    heads = columns // HEAD_DIM
    chunks = len(split_heads(heads))
    m = n // 2
    high = 8 * pl.cdiv(heads, 8)
    dma = pltpu.SemaphoreType.DMA
    vmem = pl.BlockSpec(memory_space=pltpu.VMEM)
    hbm = pl.BlockSpec(memory_space=pltpu.HBM)
    return pl.pallas_call(
        functools.partial(kernel, n),
        out_shape=jax.ShapeDtypeStruct((rows, columns), jnp.bfloat16),
        in_specs=[vmem, hbm, hbm],
        out_specs=vmem,
        scratch_shapes=[
            pltpu.VMEM((2, m, rows, columns), jnp.bfloat16),
            pltpu.VMEM((heads, depth, HEAD_DIM), jnp.bfloat16),
            pltpu.VMEM((heads, depth, HEAD_DIM), jnp.bfloat16),
            pltpu.VMEM((heads, 2, m, rows, HEAD_DIM), jnp.float32),
            pltpu.VMEM((2, m, rows, LANES), jnp.float32),
            pltpu.VMEM((heads, m, rows, HEAD_DIM), LINK),
            pltpu.VMEM((heads, m, rows, HEAD_DIM), LINK),
            pltpu.VMEM((chunks, high, m * rows), jnp.float32),
            pltpu.VMEM((chunks, high, m * rows), jnp.float32),
            pltpu.VMEM((m, heads, rows, HEAD_DIM), LINK),
            pltpu.VMEM((m, heads, rows, HEAD_DIM), LINK),
            pltpu.VMEM((m, rows, LANES), jnp.float32),
            pltpu.VMEM((m, rows, LANES), jnp.float32),
            dma((heads,)), dma((heads,)),
            dma((chunks, m)), dma((chunks, m)),
            dma((chunks, m)), dma((chunks, m)),
            dma((chunks,)), dma((chunks,)),
            dma((chunks,)), dma((chunks,)),
            dma((chunks, m)), dma((chunks, m)),
            dma((m,)), dma((m,)),
        ],
        compiler_params=pltpu.CompilerParams(
            collective_id=0, has_side_effects=True, vmem_limit_bytes=48 * 1024 * 1024
        ),
        name="attend",
    )(queries, keys, values)


def solution(mesh):
    spec = P(("groups", "seq"), "tensor")
    return jax.shard_map(
        functools.partial(body, mesh.shape["seq"]),
        mesh=mesh,
        in_specs=(spec, spec, spec),
        out_specs=spec,
        check_vma=False,
    )
```
